256 devices in a mesh: span: 32 (over z, y_hi, core), head: 8 (over x, y_lo).
Axes of the slice: x: 4, y: 4 (y_hi: 2, y_lo: 2; y = y_hi * 2 + y_lo), z: 8, core: 2. Of those that a mesh axis runs over, the one named last changes fastest.
Arguments:
- queries: bfloat16 [16384, 6144], P('span', 'head'), may hold values from -16 to 16
- stacked_key_vectors: bfloat16 [16384, 1024], P('span', 'head'), may hold values from -16 to 16
- stacked_value_vectors: bfloat16 [16384, 1024], P('span', 'head'), may hold values from -6 to 6
- out_weight: bfloat16 [6144, 6144], P('head'), may hold values from -0.625 to 0.625
- residual: bfloat16 [16384, 6144], P(('span', 'head')), may hold values from -6 to 6
- gate_table: float32 [32, 6144], replicated, may hold values from 0.25 to 1.75
- noise_step: int32 [32], replicated, may hold values from 0 to 31
- older_count: int32 [32], replicated, may hold values from 0 to 7, as said below
Outputs:
- output: bfloat16 [16384, 6144], P(('span', 'head'))
The draws below stay inside these ranges and needn't reach their ends.
Inputs may be any that keep to these rules, and one draw needn't show every extreme that they name: older_count[c] is at most c; some span has exactly 7.
All inputs are finite; a program needn't handle non-finite values.
Results may differ from the reference program's by a relative error of at most 0.014.
Values may be sent and summed in bfloat16 or wider, within the bound.
A program may use at most 64 MiB of HBM per device.

```python
import math
import jax
import jax.numpy as jnp
from jax import lax

D = 6144
QUERY_HEADS = 48
KEY_VALUE_HEADS = 8
HEAD_SIZE = 128
SPAN_TOKENS = 512
OLDER_SPAN_LIMIT = 7
STEPS = 32
SPANS = 32
WINDOW_TOKENS = 16384
N_HEAD = 8


def draw_queries(key, part):
    base_offset = 2.0 * jnp.clip(jax.random.normal(jax.random.fold_in(key, 11), (WINDOW_TOKENS, QUERY_HEADS, HEAD_SIZE), jnp.float32), -4.0, 4.0)
    return base_offset.reshape(WINDOW_TOKENS, QUERY_HEADS * HEAD_SIZE).astype(jnp.bfloat16)


def draw_stacked_key_vectors(key, part):
    base_offset = jnp.clip(jax.random.normal(jax.random.fold_in(key, 13), (WINDOW_TOKENS, KEY_VALUE_HEADS, HEAD_SIZE), jnp.float32), -4.0, 4.0)
    return base_offset.reshape(WINDOW_TOKENS, KEY_VALUE_HEADS * HEAD_SIZE).astype(jnp.bfloat16)


def draw_older_count(key, part):
    drawn = jax.random.randint(jax.random.fold_in(key, 21), (SPANS,), 0, OLDER_SPAN_LIMIT + 1)
    span_ids = jnp.arange(SPANS, dtype=jnp.int32)
    drawn = jnp.minimum(drawn, span_ids)
    picked = jax.random.randint(jax.random.fold_in(key, 22), (), OLDER_SPAN_LIMIT, SPANS)
    drawn = jnp.where(span_ids == picked, OLDER_SPAN_LIMIT, drawn)
    return drawn.astype(jnp.int32)


def plant(values, rng, low, high):
    index_at = [jax.random.randint(jax.random.fold_in(rng, axis), (), 0, length) for axis, length in enumerate(values.shape)]
    main_axis = values.shape.index(max(values.shape))
    beside = index_at[:main_axis] + [(index_at[main_axis] + 1) % values.shape[main_axis]] + index_at[main_axis + 1:]
    return values.at[tuple(index_at)].set(low).at[tuple(beside)].set(high)


def shard_levels(stream_key, extent, pieces, low, largest):
    gain, own = 1.0, jax.random.fold_in(stream_key, 6)
    for axis_at, blocks in pieces:
        draws = jnp.exp(jax.random.uniform(jax.random.fold_in(own, axis_at), (blocks,), jnp.float32, low / len(pieces), largest / len(pieces)))
        gain = gain * jnp.repeat(draws, extent[axis_at] // blocks).reshape([-1 if axis == axis_at else 1 for axis in range(len(extent))])
    return gain


def scatter_about(key, extent, spread, limit, cuts=(), kind=jnp.bfloat16):
    entries = jax.random.normal(key, extent, jnp.float32) * spread
    if len(cuts) > 0:
        entries = shard_levels(key, extent, cuts, -0.22, 0.18) * entries
    return jnp.clip(entries, min=-limit, max=limit).astype(kind)


def setup_inputs(seed: int = 0) -> dict:
    arg_keys = jax.random.split(jax.random.key(seed), 9)
    queries = draw_queries(jax.random.fold_in(arg_keys[8], 71), 0)
    stacked_key_vectors = draw_stacked_key_vectors(jax.random.fold_in(arg_keys[8], 71), 0)
    stacked_value_vectors = scatter_about(arg_keys[2], (WINDOW_TOKENS, KEY_VALUE_HEADS * HEAD_SIZE), 1.0, 6.0, ((0, 32), (1, 8)))
    out_weight = scatter_about(arg_keys[3], (QUERY_HEADS * HEAD_SIZE, D), (QUERY_HEADS * HEAD_SIZE // 64) ** -0.5, 0.625, ((0, 8),))
    residual = scatter_about(arg_keys[4], (WINDOW_TOKENS, D), 1.0, 6.0, ((0, 256),))
    gate_table = jnp.clip(jax.random.uniform(arg_keys[5], (STEPS, D), jnp.float32, 0.25, 1.75), 0.25, 1.75)
    noise_step = plant(jax.random.randint(arg_keys[6], (SPANS,), 0, STEPS), jax.random.fold_in(arg_keys[6], 1), 0, STEPS - 1).astype(jnp.int32)
    older_count = draw_older_count(jax.random.fold_in(arg_keys[8], 71), 0)
    return {"queries": queries, "stacked_key_vectors": stacked_key_vectors, "stacked_value_vectors": stacked_value_vectors, "out_weight": out_weight, "residual": residual, "gate_table": gate_table, "noise_step": noise_step, "older_count": older_count}


def reference(queries, stacked_key_vectors, stacked_value_vectors, out_weight, residual, gate_table, noise_step, older_count):
    window_length = OLDER_SPAN_LIMIT + 1
    query_group_size = QUERY_HEADS // KEY_VALUE_HEADS
    width_head = QUERY_HEADS * HEAD_SIZE // N_HEAD
    pad_amount = jnp.zeros((OLDER_SPAN_LIMIT * SPAN_TOKENS, KEY_VALUE_HEADS * HEAD_SIZE), stacked_key_vectors.dtype)
    padded_keys = jnp.concatenate([pad_amount, stacked_key_vectors], axis=0)
    padded_values = jnp.concatenate([pad_amount, stacked_value_vectors], axis=0)
    weight_groups = out_weight.astype(jnp.float32).reshape(N_HEAD, width_head, D)

    def one_span(span_idx):
        starting_row = (span_idx * SPAN_TOKENS).astype(jnp.int32)
        query_span_rows = lax.dynamic_slice_in_dim(queries, starting_row, SPAN_TOKENS, 0).reshape(SPAN_TOKENS, KEY_VALUE_HEADS, query_group_size, HEAD_SIZE)
        key_row_block = lax.dynamic_slice_in_dim(padded_keys, starting_row, window_length * SPAN_TOKENS, 0).reshape(window_length * SPAN_TOKENS, KEY_VALUE_HEADS, HEAD_SIZE)
        value_row_block = lax.dynamic_slice_in_dim(padded_values, starting_row, window_length * SPAN_TOKENS, 0).reshape(window_length * SPAN_TOKENS, KEY_VALUE_HEADS, HEAD_SIZE)
        block_of = jnp.arange(window_length * SPAN_TOKENS, dtype=jnp.int32) // SPAN_TOKENS
        distance = OLDER_SPAN_LIMIT - block_of
        visible = distance <= older_count[span_idx]

        def single_head(head_idx):
            head_queries = query_span_rows[:, head_idx].astype(jnp.float32)
            head_keys = key_row_block[:, head_idx].astype(jnp.float32)
            head_values = value_row_block[:, head_idx].astype(jnp.float32)
            scores = jnp.einsum('trd,ud->rtu', head_queries, head_keys) / math.sqrt(HEAD_SIZE)
            masked = jnp.where(visible[None, None, :], scores, -1e+30)
            row_max = lax.optimization_barrier(jnp.max(masked, axis=-1))
            weights = jnp.where(visible[None, None, :], jnp.exp(masked - row_max[..., None]), 0.0)
            row_total = lax.optimization_barrier(jnp.sum(weights, axis=-1))
            rounded = lax.optimization_barrier(weights.astype(jnp.bfloat16)).astype(jnp.float32)
            numerator = jnp.einsum('rtu,ud->rtd', rounded, head_values)
            return (numerator / row_total[..., None]).astype(jnp.bfloat16)
        head_outputs = lax.map(single_head, jnp.arange(KEY_VALUE_HEADS, dtype=jnp.int32))
        attention = head_outputs.transpose(2, 0, 1, 3).reshape(SPAN_TOKENS, QUERY_HEADS * HEAD_SIZE)
        partials = jnp.einsum('tnf,nfd->ntd', attention.astype(jnp.float32).reshape(SPAN_TOKENS, N_HEAD, width_head), weight_groups)
        partials = lax.optimization_barrier(partials.astype(jnp.bfloat16)).astype(jnp.float32)
        projected = lax.optimization_barrier(jnp.sum(partials, axis=0))
        gate_row = gate_table[noise_step[span_idx]]
        residual_rows = lax.dynamic_slice_in_dim(residual, starting_row, SPAN_TOKENS, 0).astype(jnp.float32)
        return (residual_rows + gate_row[None, :] * projected).astype(jnp.bfloat16)
    result = lax.map(one_span, jnp.arange(SPANS, dtype=jnp.int32))
    return result.reshape(WINDOW_TOKENS, D)
```

```python
import math

import jax
import jax.numpy as jnp
from jax import lax
from jax.experimental import pallas as pl
from jax.experimental.pallas import tpu as pltpu
from jax.sharding import PartitionSpec as P

MESH = pl.DeviceIdType.MESH
HEAD_SIZE = 128
BLOCKS = 8
TQ = 256
NEG = -1e30
NPAIR = 6
CX = 512
CY = 512
X_RING = 4


def kernel(
    q_hbm,
    k_hbm,
    v_hbm,
    w_hbm,
    res_hbm,
    gate_hbm,
    noise_ref,
    older_ref,
    out_ref,
    kv,
    vx,
    qv,
    wv,
    resv,
    gatev,
    m_ref,
    acc,
    att,
    px,
    rx1,
    rx2,
    sx,
    hx,
    rx3,
    py,
    ry1,
    ry2,
    ry3,
    loc_sem,
    kv_send,
    kv_recv,
    rs_send,
    rs_recv,
):
    spans = lax.axis_size("span")
    planes = spans // 4
    r = lax.axis_index("span")
    z = r // 4
    pos = r % 4
    yh = pos // 2
    c = pos % 2
    h = lax.axis_index("head")
    x = h // 2
    yl = h % 2
    xr = (x + 1) % X_RING
    xl = (x + X_RING - 1) % X_RING
    xo = (x + 2) % X_RING
    right = xr * 2 + yl
    left = xl * 2 + yl
    ypair = x * 2 + (1 - yl)
    mate = r + 1 - 2 * c
    ymate = r + 2 - 4 * yh
    heads = qv.shape[1] // HEAD_SIZE
    rows = qv.shape[0]

    def local(src, dst, index):
        return pltpu.make_async_copy(src, dst, loc_sem.at[index])

    loads = [
        local(k_hbm, kv.at[0, 0], 0),
        local(v_hbm, kv.at[0, 1], 1),
        local(q_hbm, qv, 2),
        local(w_hbm, wv, 3),
        local(res_hbm, resv, 4),
        local(gate_hbm, gatev, 5),
    ]
    for load in loads:
        load.start()

    barrier = pltpu.get_barrier_semaphore()

    def greet(device):
        pl.semaphore_signal(barrier, inc=1, device_id=device, device_id_type=MESH)

    greet({"span": mate})
    greet({"span": ymate})
    greet({"head": right})
    greet({"head": left})
    greet({"head": ypair})

    @pl.when(z < planes - 1)
    def _():
        greet({"span": r + 4})

    @pl.when(z > 0)
    def _():
        greet({"span": r - 4})

    vx[:, HEAD_SIZE:] = jnp.ones((rows, HEAD_SIZE), jnp.bfloat16)
    m_ref[...] = jnp.full(m_ref.shape, NEG, jnp.float32)
    acc[...] = jnp.zeros(acc.shape, jnp.float32)
    full = 5 + jnp.where(z < planes - 1, 1, 0) + jnp.where(z > 0, 1, 0)
    pl.semaphore_wait(barrier, full)

    def kv_copy(index, source, target, span):
        return pltpu.make_async_remote_copy(
            src_ref=kv.at[source],
            dst_ref=kv.at[target],
            send_sem=kv_send.at[index],
            recv_sem=kv_recv.at[target],
            device_id={"span": span},
            device_id_type=MESH,
        )

    up = z < planes - 1
    routes = [
        (0, up, kv_copy(0, 0, 4, r + 4)),
        (0, yh == 0, kv_copy(1, 0, 2, ymate)),
        (0, c == 0, kv_copy(2, 0, 1, mate)),
        (4, yh == 1, kv_copy(3, 4, 2, ymate)),
        (4, c >= 0, kv_copy(4, 4, 5 - 2 * c, mate)),
        (2, up, kv_copy(5, 2, 6, r + 4)),
        (2, c >= 0, kv_copy(6, 2, 3 - 2 * c, mate)),
        (3, jnp.logical_and(up, c == 0), kv_copy(7, 3, 7, r + 4)),
        (6, c >= 0, kv_copy(8, 6, 7 - 2 * c, mate)),
    ]

    loads[0].wait()
    loads[1].wait()

    def forward(slot_static):
        for source, condition, copy in routes:
            if source == slot_static:

                @pl.when(condition)
                def _(copy=copy):
                    copy.start()

    forward(0)
    loads[2].wait()

    older = older_ref[r]
    scale = math.log2(math.e) / math.sqrt(HEAD_SIZE)
    units = [(g, t) for g in range(heads) for t in range(rows // TQ)]

    def attend(slot):
        seen = slot <= older
        vx[:, :HEAD_SIZE] = kv[slot, 1]
        keys = kv[slot, 0]

        def score(unit):
            g, t = unit
            return lax.dot_general(
                qv[t * TQ : (t + 1) * TQ, g * HEAD_SIZE : (g + 1) * HEAD_SIZE],
                keys,
                (((1,), (1,)), ((), ())),
                preferred_element_type=jnp.float32,
            )

        ahead = score(units[0])
        for index, (g, t) in enumerate(units):
            s = ahead
            if index + 1 < len(units):
                ahead = score(units[index + 1])
            part = slice(t * TQ, (t + 1) * TQ)
            before = m_ref[g, part]
            top = jnp.max(s, axis=1, keepdims=True) * scale
            top = jnp.where(seen, top, NEG)
            now = jnp.maximum(before, top)
            m_ref[g, part] = now
            base = jnp.where(seen, now, -NEG)
            p = jnp.exp2(s * scale - jnp.tile(base, (1, s.shape[1] // 128)))
            alpha = jnp.exp2(before - now)
            added = jnp.dot(
                p.astype(jnp.bfloat16), vx[...], preferred_element_type=jnp.float32
            )
            acc[g, part] = acc[g, part] * jnp.tile(alpha, (1, 2)) + added

    def arrive(j, carry):
        slot0 = jnp.where(j == 0, 0, jnp.where(j < 5, 5 - j, 12 - j))
        slot1 = jnp.where(
            j == 1, 1, jnp.where(jnp.logical_or(j == 2, j == 3), j + 2, jnp.where(
                jnp.logical_or(j == 4, j == 5), j - 2, j))
        )
        slot = jnp.where(c == 0, slot0, slot1)

        @pl.when(r >= slot)
        def _():
            @pl.when(slot > 0)
            def _():
                pltpu.make_async_copy(
                    kv.at[slot], kv.at[slot], kv_recv.at[slot]
                ).wait()

            for s in (4, 2, 3, 6):

                @pl.when(slot == s)
                def _(s=s):
                    forward(s)

            attend(slot)

        return carry

    lax.fori_loop(0, BLOCKS, arrive, 0)

    for g in range(heads):
        att[:, g * HEAD_SIZE : (g + 1) * HEAD_SIZE] = (
            acc[g, :, :HEAD_SIZE] / acc[g, :, HEAD_SIZE:]
        ).astype(jnp.bfloat16)

    for load in loads[3:]:
        load.wait()

    step = noise_ref[r]

    def rs_copy(i, index, source, target, device):
        return pltpu.make_async_remote_copy(
            src_ref=source,
            dst_ref=target,
            send_sem=rs_send.at[i, index],
            recv_sem=rs_recv.at[i, index],
            device_id={"head": device},
            device_id_type=MESH,
        )

    def x1(i):
        return (
            rs_copy(i, 0, px.at[i, xo, pl.ds(0, 64)], rx1.at[i, 0], right),
            rs_copy(i, 1, px.at[i, xo, pl.ds(64, 64)], rx1.at[i, 1], left),
        )

    def x2(i):
        return (
            rs_copy(i, 2, px.at[i, xr], rx2.at[i, 0], right),
            rs_copy(i, 3, px.at[i, xl], rx2.at[i, 1], left),
        )

    def x3(i):
        return (rs_copy(i, 4, sx.at[i], rx3.at[i], ypair),)

    def y1(i):
        return (rs_copy(i, 5, py.at[i, 1 - yl], ry1.at[i], ypair),)

    def y2(i):
        return (
            rs_copy(i, 6, py.at[i, yl, xo, pl.ds(0, 32)], ry2.at[i, 0], right),
            rs_copy(i, 7, py.at[i, yl, xo, pl.ds(32, 32)], ry2.at[i, 1], left),
        )

    def y3(i):
        return (
            rs_copy(i, 8, py.at[i, yl, xr], ry3.at[i, 0], right),
            rs_copy(i, 9, py.at[i, yl, xl], ry3.at[i, 1], left),
        )

    def start(copies):
        for copy in copies:
            copy.start()

    def landed(copies):
        for copy in copies:
            copy.wait_recv()

    def f32(value):
        return value.astype(jnp.float32)

    def bf16(value):
        return value.astype(jnp.bfloat16)

    def finish(first, width, total):
        columns = pl.ds(pl.multiple_of(first, 128), width)
        gate = gatev[pl.ds(step, 1), columns]
        out_ref[:, columns] = bf16(f32(resv[:, columns]) + gate * total)

    def stage(s, carry):
        @pl.when(s < NPAIR)
        def _():
            i = s
            first = pl.multiple_of(i * (CX + CY), 128)
            wide = jnp.dot(
                att[...], wv[:, pl.ds(first, CX)], preferred_element_type=jnp.float32
            )
            px[i] = bf16(wide).reshape(X_RING, 128, CX)
            start(x1(i))
            second = pl.multiple_of(first + CX, 128)
            wide = jnp.dot(
                att[...], wv[:, pl.ds(second, CY)], preferred_element_type=jnp.float32
            )
            wide = bf16(wide).reshape(X_RING, 2, 64, CY)
            py[i, 0] = wide[:, 0]
            py[i, 1] = wide[:, 1]
            start(y1(i))

        @pl.when(jnp.logical_and(s >= 1, s < NPAIR + 1))
        def _():
            i = s - 1
            landed(x1(i))
            px[i, xr, pl.ds(0, 64)] = bf16(f32(px[i, xr, pl.ds(0, 64)]) + f32(rx1[i, 0]))
            px[i, xl, pl.ds(64, 64)] = bf16(
                f32(px[i, xl, pl.ds(64, 64)]) + f32(rx1[i, 1])
            )
            start(x2(i))
            landed(y1(i))
            py[i, yl] = bf16(f32(py[i, yl]) + f32(ry1[i]))
            start(y2(i))

        @pl.when(jnp.logical_and(s >= 2, s < NPAIR + 2))
        def _():
            i = s - 2
            landed(x2(i))
            away = pl.ds(pl.multiple_of((1 - yl) * 64, 64), 64)
            mine = pl.ds(pl.multiple_of(yl * 64, 64), 64)
            sx[i] = bf16(
                f32(px[i, x, away]) + f32(rx2[i, 0, away]) + f32(rx2[i, 1, away])
            )
            start(x3(i))
            hx[i] = f32(px[i, x, mine]) + f32(rx2[i, 0, mine]) + f32(rx2[i, 1, mine])
            landed(y2(i))
            py[i, yl, xr, pl.ds(0, 32)] = bf16(
                f32(py[i, yl, xr, pl.ds(0, 32)]) + f32(ry2[i, 0])
            )
            py[i, yl, xl, pl.ds(32, 32)] = bf16(
                f32(py[i, yl, xl, pl.ds(32, 32)]) + f32(ry2[i, 1])
            )
            start(y3(i))

        @pl.when(s >= 3)
        def _():
            i = s - 3
            landed(x3(i))
            finish(i * (CX + CY), CX, hx[i] + f32(rx3[i]))
            landed(y3(i))
            total = f32(py[i, yl, x]) + f32(ry3[i, 0]) + f32(ry3[i, 1])
            finish(i * (CX + CY) + CX, CY, total)

        return carry

    lax.fori_loop(0, NPAIR + 3, stage, 0)

    for source, condition, copy in routes:

        @pl.when(jnp.logical_and(condition, r >= source))
        def _(copy=copy):
            copy.wait_send()

    def drain(i, carry):
        for copies in (x1(i), x2(i), x3(i), y1(i), y2(i), y3(i)):
            for copy in copies:
                copy.wait_send()
        return carry

    lax.fori_loop(0, NPAIR, drain, 0)


def on_device(q, k, v, w, residual, gate_table, noise_step, older_count):
    rows, width = q.shape
    heads = width // HEAD_SIZE
    any_space = pl.BlockSpec(memory_space=pl.ANY)
    smem = pl.BlockSpec(memory_space=pltpu.SMEM)
    bf, f3 = jnp.bfloat16, jnp.float32
    flops = 2 * rows * width * (w.shape[1] + 2 * BLOCKS * rows)
    return pl.pallas_call(
        kernel,
        out_shape=jax.ShapeDtypeStruct(residual.shape, residual.dtype),
        in_specs=[any_space] * 6 + [smem] * 2,
        out_specs=pl.BlockSpec(memory_space=pltpu.VMEM),
        scratch_shapes=[
            pltpu.VMEM((BLOCKS, 2, rows, HEAD_SIZE), bf),
            pltpu.VMEM((rows, 2 * HEAD_SIZE), bf),
            pltpu.VMEM((rows, width), bf),
            pltpu.VMEM(w.shape, bf),
            pltpu.VMEM(residual.shape, bf),
            pltpu.VMEM(gate_table.shape, f3),
            pltpu.VMEM((heads, rows, 128), f3),
            pltpu.VMEM((heads, rows, 2 * HEAD_SIZE), f3),
            pltpu.VMEM((rows, width), bf),
            pltpu.VMEM((NPAIR, X_RING, 128, CX), bf),
            pltpu.VMEM((NPAIR, 2, 64, CX), bf),
            pltpu.VMEM((NPAIR, 2, 128, CX), bf),
            pltpu.VMEM((NPAIR, 64, CX), bf),
            pltpu.VMEM((NPAIR, 64, CX), f3),
            pltpu.VMEM((NPAIR, 64, CX), bf),
            pltpu.VMEM((NPAIR, 2, X_RING, 64, CY), bf),
            pltpu.VMEM((NPAIR, X_RING, 64, CY), bf),
            pltpu.VMEM((NPAIR, 2, 32, CY), bf),
            pltpu.VMEM((NPAIR, 2, 64, CY), bf),
            pltpu.SemaphoreType.DMA((6,)),
            pltpu.SemaphoreType.DMA((9,)),
            pltpu.SemaphoreType.DMA((BLOCKS,)),
            pltpu.SemaphoreType.DMA((NPAIR, 10)),
            pltpu.SemaphoreType.DMA((NPAIR, 10)),
        ],
        compiler_params=pltpu.CompilerParams(
            collective_id=0, has_side_effects=True, vmem_limit_bytes=60 * 1024 * 1024
        ),
        cost_estimate=pl.CostEstimate(
            flops=flops,
            bytes_accessed=2 * w.size,
            transcendentals=rows * BLOCKS * rows * heads,
        ),
    )(q, k, v, w, residual, gate_table, noise_step, older_count)


def solution(mesh):
    in_specs = (
        P("span", "head"),
        P("span", "head"),
        P("span", "head"),
        P("head", None),
        P(("span", "head"), None),
        P(),
        P(),
        P(),
    )
    out_specs = P(("span", "head"), None)
    return jax.shard_map(
        on_device, mesh=mesh, in_specs=in_specs, out_specs=out_specs, check_vma=False
    )
```

```python
import math

import jax
import jax.numpy as jnp
from jax import lax
from jax.experimental import pallas as pl
from jax.experimental.pallas import tpu as pltpu
from jax.sharding import PartitionSpec as P

MESH = pl.DeviceIdType.MESH
HEAD_SIZE = 128
BLOCKS = 8
HALVES = 2
AT_ONCE = 3
NEG = -1e30
GROUPS = 6
UNITS = HALVES * GROUPS
CX = 512
CY = 512
LAG = 3
X_RING = 4


def kernel(
    q_hbm,
    k_hbm,
    v_hbm,
    w_hbm,
    res_hbm,
    gate_hbm,
    noise_ref,
    older_ref,
    out_ref,
    kv,
    vx,
    qv,
    wv,
    resv,
    gatev,
    m_ref,
    acc,
    att,
    px,
    rx1,
    rx2,
    sx,
    hx,
    rx3,
    py,
    ry1,
    ry2,
    ry3,
    loc_sem,
    kv_send,
    kv_recv,
    rs_send,
    rs_recv,
):
    spans = lax.axis_size("span")
    planes = spans // 4
    r = lax.axis_index("span")
    z = r // 4
    pos = r % 4
    yh = pos // 2
    c = pos % 2
    h = lax.axis_index("head")
    x = h // 2
    yl = h % 2
    xr = (x + 1) % X_RING
    xl = (x + X_RING - 1) % X_RING
    xo = (x + 2) % X_RING
    right = xr * 2 + yl
    left = xl * 2 + yl
    ypair = x * 2 + (1 - yl)
    mate = r + 1 - 2 * c
    ymate = r + 2 - 4 * yh
    rows = kv.shape[2]
    heads = qv.shape[3] // HEAD_SIZE
    half_rows = qv.shape[1] * qv.shape[2]
    piece = qv.shape[2]

    def local(src, dst, index):
        return pltpu.make_async_copy(src, dst, loc_sem.at[index])

    loads = [
        local(k_hbm, kv.at[0, 0], 0),
        local(v_hbm, kv.at[0, 1], 1),
        local(q_hbm.at[:, 0], qv.at[0], 2),
        local(q_hbm.at[:, 1], qv.at[1], 3),
        local(w_hbm, wv, 4),
        local(res_hbm, resv, 5),
        local(gate_hbm, gatev, 6),
    ]
    for load in loads:
        load.start()

    barrier = pltpu.get_barrier_semaphore()

    def greet(device):
        pl.semaphore_signal(barrier, inc=1, device_id=device, device_id_type=MESH)

    greet({"span": mate})
    greet({"span": ymate})
    greet({"head": right})
    greet({"head": left})
    greet({"head": ypair})

    @pl.when(z < planes - 1)
    def _():
        greet({"span": r + 4})

    @pl.when(z > 0)
    def _():
        greet({"span": r - 4})

    vx[:, HEAD_SIZE:] = jnp.ones((rows, HEAD_SIZE), jnp.bfloat16)
    m_ref[...] = jnp.full(m_ref.shape, NEG, jnp.float32)
    acc[...] = jnp.zeros(acc.shape, jnp.float32)
    full = 5 + jnp.where(z < planes - 1, 1, 0) + jnp.where(z > 0, 1, 0)
    pl.semaphore_wait(barrier, full)

    def kv_copy(index, part, source, target, span):
        return pltpu.make_async_remote_copy(
            src_ref=kv.at[source, part],
            dst_ref=kv.at[target, part],
            send_sem=kv_send.at[index, part],
            recv_sem=kv_recv.at[target, part],
            device_id={"span": span},
            device_id_type=MESH,
        )

    up = z < planes - 1
    always = c >= 0
    routes = [
        (0, up, 4, r + 4),
        (0, yh == 0, 2, ymate),
        (0, c == 0, 1, mate),
        (4, yh == 1, 2, ymate),
        (4, always, 5 - 2 * c, mate),
        (2, up, 6, r + 4),
        (2, always, 3 - 2 * c, mate),
        (3, jnp.logical_and(up, c == 0), 7, r + 4),
        (6, always, 7 - 2 * c, mate),
    ]

    def forward(arrived, part):
        for index, (source, condition, target, span) in enumerate(routes):
            if source == arrived:

                @pl.when(condition)
                def _(index=index, source=source, target=target, span=span):
                    kv_copy(index, part, source, target, span).start()

    for part in (0, 1):
        loads[part].wait()
        forward(0, part)
    loads[2].wait()
    loads[3].wait()

    older = older_ref[r]
    scale = math.log2(math.e) / math.sqrt(HEAD_SIZE)

    def attend(slot, half):
        seen = slot <= older
        vx[:, :HEAD_SIZE] = kv[slot, 1]
        keys = kv[slot, 0]

        def score(g):
            mine = qv[half, :, :, g * HEAD_SIZE : (g + 1) * HEAD_SIZE]
            return lax.dot_general(
                mine.reshape(half_rows, HEAD_SIZE),
                keys,
                (((1,), (1,)), ((), ())),
                preferred_element_type=jnp.float32,
            )

        ahead = score(0)
        for g in range(heads):
            s = ahead
            if g + 1 < heads:
                ahead = score(g + 1)
            before = m_ref[half, g]
            top = jnp.max(s, axis=1, keepdims=True) * scale
            top = jnp.where(seen, top, NEG)
            now = jnp.maximum(before, top)
            m_ref[half, g] = now
            base = jnp.where(seen, now, -NEG)
            p = jnp.exp2(s * scale - jnp.tile(base, (1, s.shape[1] // 128)))
            alpha = jnp.exp2(before - now)
            added = jnp.dot(
                p.astype(jnp.bfloat16), vx[...], preferred_element_type=jnp.float32
            )
            acc[half, g] = acc[half, g] * jnp.tile(alpha, (1, 2)) + added

    def packed(slots):
        return sum(slot * 8**place for place, slot in enumerate(slots))

    orders = ([0, 4, 3, 2, 1, 7, 6, 5], [0, 1, 4, 5, 2, 3, 6, 7])

    def pick(slots0, slots1):
        return jnp.where(c == 0, packed(slots0), packed(slots1))

    def landed_kv(slot, part):
        @pl.when(slot > 0)
        def _():
            pltpu.make_async_copy(
                kv.at[slot, part], kv.at[slot, part], kv_recv.at[slot, part]
            ).wait()

        for s in (4, 2, 3, 6):

            @pl.when(slot == s)
            def _(s=s):
                forward(s, part)

    def arrive(t, carry):
        left_over, previous = carry
        slot = left_over % 8
        there = r >= slot

        @pl.when(there)
        def _():
            landed_kv(slot, 0)

        fill = jnp.logical_and(t >= 1, t <= AT_ONCE)

        @pl.when(jnp.logical_and(fill, r >= previous))
        def _():
            attend(previous, 1)

        @pl.when(there)
        def _():
            landed_kv(slot, 1)
            attend(slot, 0)

        return left_over // 8, slot

    lax.fori_loop(0, BLOCKS, arrive, (pick(*orders), jnp.int32(0)))

    def settle(half):
        for g in range(heads):
            att[half, :, g * HEAD_SIZE : (g + 1) * HEAD_SIZE] = (
                acc[half, g, :, :HEAD_SIZE] / acc[half, g, :, HEAD_SIZE:]
            ).astype(jnp.bfloat16)

    settle(0)
    for load in loads[4:]:
        load.wait()

    step = noise_ref[r]

    def rs_copy(i, index, source, target, device):
        return pltpu.make_async_remote_copy(
            src_ref=source,
            dst_ref=target,
            send_sem=rs_send.at[i, index],
            recv_sem=rs_recv.at[i, index],
            device_id={"head": device},
            device_id_type=MESH,
        )

    def x1(i):
        return (
            rs_copy(i, 0, px.at[i, xo, pl.ds(0, piece)], rx1.at[i, 0], right),
            rs_copy(i, 1, px.at[i, xo, pl.ds(piece, piece)], rx1.at[i, 1], left),
        )

    def x2(i):
        return (
            rs_copy(i, 2, px.at[i, xr], rx2.at[i, 0], right),
            rs_copy(i, 3, px.at[i, xl], rx2.at[i, 1], left),
        )

    def x3(i):
        return (rs_copy(i, 4, sx.at[i], rx3.at[i], ypair),)

    def y1(i):
        return (rs_copy(i, 5, py.at[i, 1 - yl], ry1.at[i], ypair),)

    def y2(i):
        return (
            rs_copy(i, 6, py.at[i, yl, xo, pl.ds(0, piece // 2)], ry2.at[i, 0], right),
            rs_copy(i, 7, py.at[i, yl, xo, pl.ds(piece // 2, piece // 2)], ry2.at[i, 1], left),
        )

    def y3(i):
        return (
            rs_copy(i, 8, py.at[i, yl, xr], ry3.at[i, 0], right),
            rs_copy(i, 9, py.at[i, yl, xl], ry3.at[i, 1], left),
        )

    def start(copies):
        for copy in copies:
            copy.start()

    def landed(copies):
        for copy in copies:
            copy.wait_recv()

    def f32(value):
        return value.astype(jnp.float32)

    def bf16(value):
        return value.astype(jnp.bfloat16)

    def finish(i, shift, width, total):
        first = (i % GROUPS) * (CX + CY) + shift
        columns = pl.ds(pl.multiple_of(first, 128), width)
        mine = pl.ds(pl.multiple_of((i // GROUPS) * piece, piece), piece)
        gate = gatev[pl.ds(step, 1), columns]
        out_ref[mine, columns] = bf16(f32(resv[mine, columns]) + gate * total)

    low = pl.ds(0, piece)
    high = pl.ds(piece, piece)
    low2 = pl.ds(0, piece // 2)
    high2 = pl.ds(piece // 2, piece // 2)
    away = pl.ds(pl.multiple_of((1 - yl) * piece, piece), piece)
    kept = pl.ds(pl.multiple_of(yl * piece, piece), piece)

    def stage(s, later):
        slot = later % 8

        @pl.when(s < UNITS)
        def _():
            i = s
            half = i // GROUPS
            first = pl.multiple_of((i % GROUPS) * (CX + CY), 128)
            wide = jnp.dot(
                att[half], wv[:, pl.ds(first, CX)], preferred_element_type=jnp.float32
            )
            px[i] = bf16(wide).reshape(X_RING, 2 * piece, CX)
            start(x1(i))
            second = pl.multiple_of(first + CX, 128)
            wide = jnp.dot(
                att[half], wv[:, pl.ds(second, CY)], preferred_element_type=jnp.float32
            )
            wide = bf16(wide).reshape(X_RING, 2, piece, CY)
            py[i, 0] = wide[:, 0]
            py[i, 1] = wide[:, 1]
            start(y1(i))

        @pl.when(jnp.logical_and(s < BLOCKS - AT_ONCE, r >= slot))
        def _():
            attend(slot, 1)

        @pl.when(s == BLOCKS - AT_ONCE)
        def _():
            settle(1)

        @pl.when(jnp.logical_and(s >= LAG, s < UNITS + LAG))
        def _():
            i = s - LAG
            landed(x1(i))
            px[i, xr, low] = bf16(f32(px[i, xr, low]) + f32(rx1[i, 0]))
            px[i, xl, high] = bf16(f32(px[i, xl, high]) + f32(rx1[i, 1]))
            start(x2(i))
            landed(y1(i))
            py[i, yl] = bf16(f32(py[i, yl]) + f32(ry1[i]))
            start(y2(i))

        @pl.when(jnp.logical_and(s >= 2 * LAG, s < UNITS + 2 * LAG))
        def _():
            i = s - 2 * LAG
            landed(x2(i))
            sx[i] = bf16(
                f32(px[i, x, away]) + f32(rx2[i, 0, away]) + f32(rx2[i, 1, away])
            )
            start(x3(i))
            hx[i] = f32(px[i, x, kept]) + f32(rx2[i, 0, kept]) + f32(rx2[i, 1, kept])
            landed(y2(i))
            py[i, yl, xr, low2] = bf16(f32(py[i, yl, xr, low2]) + f32(ry2[i, 0]))
            py[i, yl, xl, high2] = bf16(f32(py[i, yl, xl, high2]) + f32(ry2[i, 1]))
            start(y3(i))

        @pl.when(s >= 3 * LAG)
        def _():
            i = s - 3 * LAG
            landed(x3(i))
            finish(i, 0, CX, hx[i] + f32(rx3[i]))
            landed(y3(i))
            total = f32(py[i, yl, x]) + f32(ry3[i, 0]) + f32(ry3[i, 1])
            finish(i, CX, CY, total)

        return later // 8

    lax.fori_loop(0, UNITS + 3 * LAG, stage, pick(orders[0][AT_ONCE:], orders[1][AT_ONCE:]))

    for index, (source, condition, target, span) in enumerate(routes):

        @pl.when(jnp.logical_and(condition, r >= source))
        def _(index=index, source=source, target=target, span=span):
            for part in (0, 1):
                kv_copy(index, part, source, target, span).wait_send()

    def drain(i, carry):
        for copies in (x1(i), x2(i), x3(i), y1(i), y2(i), y3(i)):
            for copy in copies:
                copy.wait_send()
        return carry

    lax.fori_loop(0, UNITS, drain, 0)


def on_device(q, k, v, w, residual, gate_table, noise_step, older_count):
    rows, width = q.shape
    heads = width // HEAD_SIZE
    half_rows = rows // HALVES
    piece = residual.shape[0] // HALVES
    q = q.reshape(half_rows // piece, HALVES, piece, width)
    any_space = pl.BlockSpec(memory_space=pl.ANY)
    smem = pl.BlockSpec(memory_space=pltpu.SMEM)
    bf, f3 = jnp.bfloat16, jnp.float32
    flops = 2 * rows * width * (w.shape[1] + 2 * BLOCKS * rows)
    return pl.pallas_call(
        kernel,
        out_shape=pltpu.VMEM(residual.shape, residual.dtype),
        in_specs=[any_space] * 6 + [smem] * 2,
        out_specs=pl.BlockSpec(memory_space=pltpu.VMEM),
        scratch_shapes=[
            pltpu.VMEM((BLOCKS, 2, rows, HEAD_SIZE), bf),
            pltpu.VMEM((rows, 2 * HEAD_SIZE), bf),
            pltpu.VMEM((HALVES, half_rows // piece, piece, width), bf),
            pltpu.VMEM(w.shape, bf),
            pltpu.VMEM(residual.shape, bf),
            pltpu.VMEM(gate_table.shape, f3),
            pltpu.VMEM((HALVES, heads, half_rows, 128), f3),
            pltpu.VMEM((HALVES, heads, half_rows, 2 * HEAD_SIZE), f3),
            pltpu.VMEM((HALVES, half_rows, width), bf),
            pltpu.VMEM((UNITS, X_RING, 2 * piece, CX), bf),
            pltpu.VMEM((UNITS, 2, piece, CX), bf),
            pltpu.VMEM((UNITS, 2, 2 * piece, CX), bf),
            pltpu.VMEM((UNITS, piece, CX), bf),
            pltpu.VMEM((UNITS, piece, CX), f3),
            pltpu.VMEM((UNITS, piece, CX), bf),
            pltpu.VMEM((UNITS, 2, X_RING, piece, CY), bf),
            pltpu.VMEM((UNITS, X_RING, piece, CY), bf),
            pltpu.VMEM((UNITS, 2, piece // 2, CY), bf),
            pltpu.VMEM((UNITS, 2, piece, CY), bf),
            pltpu.SemaphoreType.DMA((7,)),
            pltpu.SemaphoreType.DMA((9, 2)),
            pltpu.SemaphoreType.DMA((BLOCKS, 2)),
            pltpu.SemaphoreType.DMA((UNITS, 10)),
            pltpu.SemaphoreType.DMA((UNITS, 10)),
        ],
        compiler_params=pltpu.CompilerParams(
            collective_id=0, has_side_effects=True, vmem_limit_bytes=60 * 1024 * 1024
        ),
        cost_estimate=pl.CostEstimate(
            flops=flops,
            bytes_accessed=2 * w.size,
            transcendentals=rows * BLOCKS * rows * heads,
        ),
    )(q, k, v, w, residual, gate_table, noise_step, older_count)


def solution(mesh):
    in_specs = (
        P("span", "head"),
        P("span", "head"),
        P("span", "head"),
        P("head", None),
        P(("span", "head"), None),
        P(),
        P(),
        P(),
    )
    out_specs = P(("span", "head"), None)
    return jax.shard_map(
        on_device, mesh=mesh, in_specs=in_specs, out_specs=out_specs, check_vma=False
    )
```

```python
import math

import jax
import jax.numpy as jnp
from jax import lax
from jax.experimental import pallas as pl
from jax.experimental.pallas import tpu as pltpu
from jax.sharding import PartitionSpec as P

MESH = pl.DeviceIdType.MESH
HEAD_SIZE = 128
BLOCKS = 8
HALVES = 2
AT_ONCE = 3
NEG = -1e30
GROUPS = 6
UNITS = HALVES * GROUPS
CX = 512
CY = 512
LAG = 3
X_RING = 4


def kernel(
    q_hbm,
    k_hbm,
    v_hbm,
    w_hbm,
    res_hbm,
    gate_hbm,
    noise_ref,
    older_ref,
    out_ref,
    kv,
    vx,
    qv,
    wv,
    resv,
    gatev,
    m_ref,
    acc,
    att,
    px,
    rx1,
    rx2,
    sx,
    hx,
    rx3,
    py,
    ry1,
    ry2,
    ry3,
    loc_sem,
    kv_send,
    kv_recv,
    rs_send,
    rs_recv,
):
    spans = lax.axis_size("span")
    planes = spans // 4
    r = lax.axis_index("span")
    z = r // 4
    pos = r % 4
    yh = pos // 2
    c = pos % 2
    h = lax.axis_index("head")
    x = h // 2
    yl = h % 2
    xr = (x + 1) % X_RING
    xl = (x + X_RING - 1) % X_RING
    xo = (x + 2) % X_RING
    right = xr * 2 + yl
    left = xl * 2 + yl
    ypair = x * 2 + (1 - yl)
    mate = r + 1 - 2 * c
    ymate = r + 2 - 4 * yh
    rows = kv.shape[2]
    heads = qv.shape[3] // HEAD_SIZE
    half_rows = qv.shape[1] * qv.shape[2]
    piece = qv.shape[2]

    def local(src, dst, index):
        return pltpu.make_async_copy(src, dst, loc_sem.at[index])

    loads = [
        local(k_hbm, kv.at[0, 0], 0),
        local(v_hbm, kv.at[0, 1], 1),
        local(q_hbm.at[:, 0], qv.at[0], 2),
        local(q_hbm.at[:, 1], qv.at[1], 3),
        local(w_hbm, wv, 4),
        local(res_hbm, resv, 5),
        local(gate_hbm, gatev, 6),
    ]
    for load in loads:
        load.start()

    barrier = pltpu.get_barrier_semaphore()

    def greet(device):
        pl.semaphore_signal(barrier, inc=1, device_id=device, device_id_type=MESH)

    greet({"span": mate})
    greet({"span": ymate})
    greet({"head": right})
    greet({"head": left})
    greet({"head": ypair})

    @pl.when(z < planes - 1)
    def _():
        greet({"span": r + 4})

    @pl.when(z > 0)
    def _():
        greet({"span": r - 4})

    @pl.when(jnp.logical_and(c == 1, z < planes - 1))
    def _():
        greet({"span": r + 3})

    @pl.when(jnp.logical_and(c == 0, z > 0))
    def _():
        greet({"span": r - 3})

    vx[:, HEAD_SIZE:] = jnp.ones((rows, HEAD_SIZE), jnp.bfloat16)
    m_ref[...] = jnp.full(m_ref.shape, NEG, jnp.float32)
    acc[...] = jnp.zeros(acc.shape, jnp.float32)
    above = jnp.where(z < planes - 1, 1, 0)
    below = jnp.where(z > 0, 1, 0)
    full = 5 + above + below + jnp.where(c == 1, above, below)
    pl.semaphore_wait(barrier, full)

    def kv_copy(index, part, source, target, span):
        return pltpu.make_async_remote_copy(
            src_ref=kv.at[source, part],
            dst_ref=kv.at[target, part],
            send_sem=kv_send.at[index, part],
            recv_sem=kv_recv.at[target, part],
            device_id={"span": span},
            device_id_type=MESH,
        )

    up = z < planes - 1
    always = c >= 0
    routes = [
        (0, up, 4, r + 4),
        (0, yh == 0, 2, ymate),
        (0, c == 0, 1, mate),
        (4, yh == 1, 2, ymate),
        (4, always, 5 - 2 * c, mate),
        (4, jnp.logical_and(up, c == 1), 7, r + 3),
        (2, up, 6, r + 4),
        (2, always, 3 - 2 * c, mate),
        (6, always, 7 - 2 * c, mate),
    ]

    def forward(arrived, part):
        for index, (source, condition, target, span) in enumerate(routes):
            if source == arrived:

                @pl.when(condition)
                def _(index=index, source=source, target=target, span=span):
                    kv_copy(index, part, source, target, span).start()

    for part in (0, 1):
        loads[part].wait()
        forward(0, part)
    loads[2].wait()
    loads[3].wait()

    older = older_ref[r]
    scale = math.log2(math.e) / math.sqrt(HEAD_SIZE)

    def attend(slot, half):
        seen = slot <= older
        vx[:, :HEAD_SIZE] = kv[slot, 1]
        keys = kv[slot, 0]

        def score(g):
            mine = qv[half, :, :, g * HEAD_SIZE : (g + 1) * HEAD_SIZE]
            return lax.dot_general(
                mine.reshape(half_rows, HEAD_SIZE),
                keys,
                (((1,), (1,)), ((), ())),
                preferred_element_type=jnp.float32,
            )

        ahead = score(0)
        for g in range(heads):
            s = ahead
            if g + 1 < heads:
                ahead = score(g + 1)
            before = m_ref[half, g]
            top = jnp.max(s, axis=1, keepdims=True) * scale
            top = jnp.where(seen, top, NEG)
            now = jnp.maximum(before, top)
            m_ref[half, g] = now
            base = jnp.where(seen, now, -NEG)
            p = jnp.exp2(s * scale - jnp.tile(base, (1, s.shape[1] // 128)))
            alpha = jnp.exp2(before - now)
            added = jnp.dot(
                p.astype(jnp.bfloat16), vx[...], preferred_element_type=jnp.float32
            )
            acc[half, g] = acc[half, g] * jnp.tile(alpha, (1, 2)) + added

    def packed(slots):
        return sum(slot * 8**place for place, slot in enumerate(slots))

    orders = ([0, 4, 3, 2, 7, 1, 6, 5], [0, 1, 4, 5, 2, 3, 6, 7])

    def pick(slots0, slots1):
        return jnp.where(c == 0, packed(slots0), packed(slots1))

    def landed_kv(slot, part):
        @pl.when(slot > 0)
        def _():
            pltpu.make_async_copy(
                kv.at[slot, part], kv.at[slot, part], kv_recv.at[slot, part]
            ).wait()

        for s in (4, 2, 6):

            @pl.when(slot == s)
            def _(s=s):
                forward(s, part)

    def arrive(t, carry):
        left_over, previous = carry
        slot = left_over % 8
        there = r >= slot

        @pl.when(there)
        def _():
            landed_kv(slot, 0)

        fill = jnp.logical_and(t >= 1, t <= AT_ONCE)

        @pl.when(jnp.logical_and(fill, r >= previous))
        def _():
            attend(previous, 1)

        @pl.when(there)
        def _():
            landed_kv(slot, 1)
            attend(slot, 0)

        return left_over // 8, slot

    lax.fori_loop(0, BLOCKS, arrive, (pick(*orders), jnp.int32(0)))

    def settle(half):
        for g in range(heads):
            att[half, :, g * HEAD_SIZE : (g + 1) * HEAD_SIZE] = (
                acc[half, g, :, :HEAD_SIZE] / acc[half, g, :, HEAD_SIZE:]
            ).astype(jnp.bfloat16)

    settle(0)
    for load in loads[4:]:
        load.wait()

    step = noise_ref[r]

    def rs_copy(i, index, source, target, device):
        return pltpu.make_async_remote_copy(
            src_ref=source,
            dst_ref=target,
            send_sem=rs_send.at[i, index],
            recv_sem=rs_recv.at[i, index],
            device_id={"head": device},
            device_id_type=MESH,
        )

    def x1(i):
        return (
            rs_copy(i, 0, px.at[i, xo, pl.ds(0, piece)], rx1.at[i, 0], right),
            rs_copy(i, 1, px.at[i, xo, pl.ds(piece, piece)], rx1.at[i, 1], left),
        )

    def x2(i):
        return (
            rs_copy(i, 2, px.at[i, xr], rx2.at[i, 0], right),
            rs_copy(i, 3, px.at[i, xl], rx2.at[i, 1], left),
        )

    def x3(i):
        return (rs_copy(i, 4, sx.at[i], rx3.at[i], ypair),)

    def y1(i):
        return (rs_copy(i, 5, py.at[i, 1 - yl], ry1.at[i], ypair),)

    def y2(i):
        return (
            rs_copy(i, 6, py.at[i, yl, xo, pl.ds(0, piece // 2)], ry2.at[i, 0], right),
            rs_copy(i, 7, py.at[i, yl, xo, pl.ds(piece // 2, piece // 2)], ry2.at[i, 1], left),
        )

    def y3(i):
        return (
            rs_copy(i, 8, py.at[i, yl, xr], ry3.at[i, 0], right),
            rs_copy(i, 9, py.at[i, yl, xl], ry3.at[i, 1], left),
        )

    def start(copies):
        for copy in copies:
            copy.start()

    def landed(copies):
        for copy in copies:
            copy.wait_recv()

    def f32(value):
        return value.astype(jnp.float32)

    def bf16(value):
        return value.astype(jnp.bfloat16)

    def finish(i, shift, width, total):
        first = (i % GROUPS) * (CX + CY) + shift
        columns = pl.ds(pl.multiple_of(first, 128), width)
        mine = pl.ds(pl.multiple_of((i // GROUPS) * piece, piece), piece)
        gate = gatev[pl.ds(step, 1), columns]
        out_ref[mine, columns] = bf16(f32(resv[mine, columns]) + gate * total)

    low = pl.ds(0, piece)
    high = pl.ds(piece, piece)
    low2 = pl.ds(0, piece // 2)
    high2 = pl.ds(piece // 2, piece // 2)
    away = pl.ds(pl.multiple_of((1 - yl) * piece, piece), piece)
    kept = pl.ds(pl.multiple_of(yl * piece, piece), piece)

    def stage(s, later):
        slot = later % 8

        @pl.when(s < UNITS)
        def _():
            i = s
            half = i // GROUPS
            first = pl.multiple_of((i % GROUPS) * (CX + CY), 128)
            second = pl.multiple_of(first + CX, 128)
            wide = jnp.dot(
                att[half], wv[:, pl.ds(second, CY)], preferred_element_type=jnp.float32
            )
            wide = bf16(wide).reshape(X_RING, 2, piece, CY)
            py[i, 0] = wide[:, 0]
            py[i, 1] = wide[:, 1]
            start(y1(i))
            wide = jnp.dot(
                att[half], wv[:, pl.ds(first, CX)], preferred_element_type=jnp.float32
            )
            px[i] = bf16(wide).reshape(X_RING, 2 * piece, CX)
            start(x1(i))

        @pl.when(jnp.logical_and(s < BLOCKS - AT_ONCE, r >= slot))
        def _():
            attend(slot, 1)

        @pl.when(s == BLOCKS - AT_ONCE)
        def _():
            settle(1)

        @pl.when(jnp.logical_and(s >= LAG, s < UNITS + LAG))
        def _():
            i = s - LAG
            landed(x1(i))
            px[i, xr, low] = bf16(f32(px[i, xr, low]) + f32(rx1[i, 0]))
            px[i, xl, high] = bf16(f32(px[i, xl, high]) + f32(rx1[i, 1]))
            start(x2(i))
            landed(y1(i))
            py[i, yl] = bf16(f32(py[i, yl]) + f32(ry1[i]))
            start(y2(i))

        @pl.when(jnp.logical_and(s >= 2 * LAG, s < UNITS + 2 * LAG))
        def _():
            i = s - 2 * LAG
            landed(x2(i))
            sx[i] = bf16(
                f32(px[i, x, away]) + f32(rx2[i, 0, away]) + f32(rx2[i, 1, away])
            )
            start(x3(i))
            hx[i] = f32(px[i, x, kept]) + f32(rx2[i, 0, kept]) + f32(rx2[i, 1, kept])
            landed(y2(i))
            py[i, yl, xr, low2] = bf16(f32(py[i, yl, xr, low2]) + f32(ry2[i, 0]))
            py[i, yl, xl, high2] = bf16(f32(py[i, yl, xl, high2]) + f32(ry2[i, 1]))
            start(y3(i))

        @pl.when(s >= 3 * LAG)
        def _():
            i = s - 3 * LAG
            landed(x3(i))
            finish(i, 0, CX, hx[i] + f32(rx3[i]))
            landed(y3(i))
            total = f32(py[i, yl, x]) + f32(ry3[i, 0]) + f32(ry3[i, 1])
            finish(i, CX, CY, total)

        return later // 8

    lax.fori_loop(0, UNITS + 3 * LAG, stage, pick(orders[0][AT_ONCE:], orders[1][AT_ONCE:]))

    for index, (source, condition, target, span) in enumerate(routes):

        @pl.when(jnp.logical_and(condition, r >= source))
        def _(index=index, source=source, target=target, span=span):
            for part in (0, 1):
                kv_copy(index, part, source, target, span).wait_send()

    def drain(i, carry):
        for copies in (x1(i), x2(i), x3(i), y1(i), y2(i), y3(i)):
            for copy in copies:
                copy.wait_send()
        return carry

    lax.fori_loop(0, UNITS, drain, 0)


def on_device(q, k, v, w, residual, gate_table, noise_step, older_count):
    rows, width = q.shape
    heads = width // HEAD_SIZE
    half_rows = rows // HALVES
    piece = residual.shape[0] // HALVES
    q = q.reshape(half_rows // piece, HALVES, piece, width)
    any_space = pl.BlockSpec(memory_space=pl.ANY)
    smem = pl.BlockSpec(memory_space=pltpu.SMEM)
    bf, f3 = jnp.bfloat16, jnp.float32
    flops = 2 * rows * width * (w.shape[1] + 2 * BLOCKS * rows)
    return pl.pallas_call(
        kernel,
        out_shape=pltpu.VMEM(residual.shape, residual.dtype),
        in_specs=[any_space] * 6 + [smem] * 2,
        out_specs=pl.BlockSpec(memory_space=pltpu.VMEM),
        scratch_shapes=[
            pltpu.VMEM((BLOCKS, 2, rows, HEAD_SIZE), bf),
            pltpu.VMEM((rows, 2 * HEAD_SIZE), bf),
            pltpu.VMEM((HALVES, half_rows // piece, piece, width), bf),
            pltpu.VMEM(w.shape, bf),
            pltpu.VMEM(residual.shape, bf),
            pltpu.VMEM(gate_table.shape, f3),
            pltpu.VMEM((HALVES, heads, half_rows, 128), f3),
            pltpu.VMEM((HALVES, heads, half_rows, 2 * HEAD_SIZE), f3),
            pltpu.VMEM((HALVES, half_rows, width), bf),
            pltpu.VMEM((UNITS, X_RING, 2 * piece, CX), bf),
            pltpu.VMEM((UNITS, 2, piece, CX), bf),
            pltpu.VMEM((UNITS, 2, 2 * piece, CX), bf),
            pltpu.VMEM((UNITS, piece, CX), bf),
            pltpu.VMEM((UNITS, piece, CX), f3),
            pltpu.VMEM((UNITS, piece, CX), bf),
            pltpu.VMEM((UNITS, 2, X_RING, piece, CY), bf),
            pltpu.VMEM((UNITS, X_RING, piece, CY), bf),
            pltpu.VMEM((UNITS, 2, piece // 2, CY), bf),
            pltpu.VMEM((UNITS, 2, piece, CY), bf),
            pltpu.SemaphoreType.DMA((7,)),
            pltpu.SemaphoreType.DMA((9, 2)),
            pltpu.SemaphoreType.DMA((BLOCKS, 2)),
            pltpu.SemaphoreType.DMA((UNITS, 10)),
            pltpu.SemaphoreType.DMA((UNITS, 10)),
        ],
        compiler_params=pltpu.CompilerParams(
            collective_id=0, has_side_effects=True, vmem_limit_bytes=60 * 1024 * 1024
        ),
        cost_estimate=pl.CostEstimate(
            flops=flops,
            bytes_accessed=2 * w.size,
            transcendentals=rows * BLOCKS * rows * heads,
        ),
    )(q, k, v, w, residual, gate_table, noise_step, older_count)


def solution(mesh):
    in_specs = (
        P("span", "head"),
        P("span", "head"),
        P("span", "head"),
        P("head", None),
        P(("span", "head"), None),
        P(),
        P(),
        P(),
    )
    out_specs = P(("span", "head"), None)
    return jax.shard_map(
        on_device, mesh=mesh, in_specs=in_specs, out_specs=out_specs, check_vma=False
    )
```

```python
import math

import jax
import jax.numpy as jnp
from jax import lax
from jax.experimental import pallas as pl
from jax.experimental.pallas import tpu as pltpu
from jax.sharding import PartitionSpec as P

MESH = pl.DeviceIdType.MESH
HEAD_SIZE = 128
BLOCKS = 8
HALVES = 2
AT_ONCE = 3
NEG = -1e30
GROUPS = 6
UNITS = HALVES * GROUPS
CX = 640
CY = 384
LAG = 3
X_RING = 4


def kernel(
    q_hbm,
    k_hbm,
    v_hbm,
    w_hbm,
    res_hbm,
    gate_hbm,
    noise_ref,
    older_ref,
    out_ref,
    kv,
    vx,
    qv,
    wv,
    resv,
    gatev,
    m_ref,
    acc,
    att,
    px,
    rx1,
    rx2,
    sx,
    hx,
    rx3,
    py,
    ry1,
    ry2,
    ry3,
    loc_sem,
    kv_send,
    kv_recv,
    rs_send,
    rs_recv,
):
    spans = lax.axis_size("span")
    planes = spans // 4
    r = lax.axis_index("span")
    z = r // 4
    pos = r % 4
    yh = pos // 2
    c = pos % 2
    h = lax.axis_index("head")
    x = h // 2
    yl = h % 2
    xr = (x + 1) % X_RING
    xl = (x + X_RING - 1) % X_RING
    xo = (x + 2) % X_RING
    right = xr * 2 + yl
    left = xl * 2 + yl
    ypair = x * 2 + (1 - yl)
    mate = r + 1 - 2 * c
    ymate = r + 2 - 4 * yh
    rows = kv.shape[2]
    heads = qv.shape[3] // HEAD_SIZE
    half_rows = qv.shape[1] * qv.shape[2]
    piece = qv.shape[2]

    def local(src, dst, index):
        return pltpu.make_async_copy(src, dst, loc_sem.at[index])

    loads = [
        local(k_hbm, kv.at[0, 0], 0),
        local(v_hbm, kv.at[0, 1], 1),
        local(q_hbm.at[:, 0], qv.at[0], 2),
        local(q_hbm.at[:, 1], qv.at[1], 3),
        local(w_hbm, wv, 4),
        local(res_hbm, resv, 5),
        local(gate_hbm, gatev, 6),
    ]
    for load in loads:
        load.start()

    barrier = pltpu.get_barrier_semaphore()

    def greet(device):
        pl.semaphore_signal(barrier, inc=1, device_id=device, device_id_type=MESH)

    greet({"span": mate})
    greet({"span": ymate})
    greet({"head": right})
    greet({"head": left})
    greet({"head": ypair})

    @pl.when(z < planes - 1)
    def _():
        greet({"span": r + 4})

    @pl.when(z > 0)
    def _():
        greet({"span": r - 4})

    @pl.when(jnp.logical_and(c == 1, z < planes - 1))
    def _():
        greet({"span": r + 3})

    @pl.when(jnp.logical_and(c == 0, z > 0))
    def _():
        greet({"span": r - 3})

    vx[:, HEAD_SIZE:] = jnp.ones((rows, HEAD_SIZE), jnp.bfloat16)
    m_ref[...] = jnp.full(m_ref.shape, NEG, jnp.float32)
    acc[...] = jnp.zeros(acc.shape, jnp.float32)
    above = jnp.where(z < planes - 1, 1, 0)
    below = jnp.where(z > 0, 1, 0)
    full = 5 + above + below + jnp.where(c == 1, above, below)
    pl.semaphore_wait(barrier, full)

    def kv_copy(index, part, source, target, span):
        return pltpu.make_async_remote_copy(
            src_ref=kv.at[source, part],
            dst_ref=kv.at[target, part],
            send_sem=kv_send.at[index, part],
            recv_sem=kv_recv.at[target, part],
            device_id={"span": span},
            device_id_type=MESH,
        )

    up = z < planes - 1
    always = c >= 0
    routes = [
        (0, up, 4, r + 4),
        (0, yh == 0, 2, ymate),
        (0, c == 0, 1, mate),
        (4, yh == 1, 2, ymate),
        (4, always, 5 - 2 * c, mate),
        (4, jnp.logical_and(up, c == 1), 7, r + 3),
        (2, up, 6, r + 4),
        (2, always, 3 - 2 * c, mate),
        (6, always, 7 - 2 * c, mate),
    ]

    def forward(arrived, part):
        for index, (source, condition, target, span) in enumerate(routes):
            if source == arrived:

                @pl.when(condition)
                def _(index=index, source=source, target=target, span=span):
                    kv_copy(index, part, source, target, span).start()

    for part in (0, 1):
        loads[part].wait()
        forward(0, part)
    loads[2].wait()
    loads[3].wait()

    older = older_ref[r]
    scale = math.log2(math.e) / math.sqrt(HEAD_SIZE)

    def attend(slot, half):
        seen = slot <= older
        vx[:, :HEAD_SIZE] = kv[slot, 1]
        keys = kv[slot, 0]

        def score(g):
            mine = qv[half, :, :, g * HEAD_SIZE : (g + 1) * HEAD_SIZE]
            return lax.dot_general(
                mine.reshape(half_rows, HEAD_SIZE),
                keys,
                (((1,), (1,)), ((), ())),
                preferred_element_type=jnp.float32,
            )

        ahead = score(0)
        for g in range(heads):
            s = ahead
            if g + 1 < heads:
                ahead = score(g + 1)
            before = m_ref[half, g]
            top = jnp.max(s, axis=1, keepdims=True) * scale
            top = jnp.where(seen, top, NEG)
            now = jnp.maximum(before, top)
            m_ref[half, g] = now
            base = jnp.where(seen, now, -NEG)
            p = jnp.exp2(s * scale - jnp.tile(base, (1, s.shape[1] // 128)))
            alpha = jnp.exp2(before - now)
            added = jnp.dot(
                p.astype(jnp.bfloat16), vx[...], preferred_element_type=jnp.float32
            )
            acc[half, g] = acc[half, g] * jnp.tile(alpha, (1, 2)) + added

    def packed(slots):
        return sum(slot * 8**place for place, slot in enumerate(slots))

    orders = ([0, 4, 3, 2, 7, 1, 6, 5], [0, 1, 4, 5, 2, 3, 6, 7])

    def pick(slots0, slots1):
        return jnp.where(c == 0, packed(slots0), packed(slots1))

    def landed_kv(slot, part):
        @pl.when(slot > 0)
        def _():
            pltpu.make_async_copy(
                kv.at[slot, part], kv.at[slot, part], kv_recv.at[slot, part]
            ).wait()

        for s in (4, 2, 6):

            @pl.when(slot == s)
            def _(s=s):
                forward(s, part)

    def arrive(t, carry):
        left_over, previous = carry
        slot = left_over % 8
        there = r >= slot

        @pl.when(there)
        def _():
            landed_kv(slot, 0)

        fill = jnp.logical_and(t >= 1, t <= AT_ONCE)

        @pl.when(jnp.logical_and(fill, r >= previous))
        def _():
            attend(previous, 1)

        @pl.when(there)
        def _():
            landed_kv(slot, 1)
            attend(slot, 0)

        return left_over // 8, slot

    lax.fori_loop(0, BLOCKS, arrive, (pick(*orders), jnp.int32(0)))

    def settle(half):
        for g in range(heads):
            att[half, :, g * HEAD_SIZE : (g + 1) * HEAD_SIZE] = (
                acc[half, g, :, :HEAD_SIZE] / acc[half, g, :, HEAD_SIZE:]
            ).astype(jnp.bfloat16)

    settle(0)
    for load in loads[4:]:
        load.wait()

    step = noise_ref[r]

    def rs_copy(i, index, source, target, device):
        return pltpu.make_async_remote_copy(
            src_ref=source,
            dst_ref=target,
            send_sem=rs_send.at[i, index],
            recv_sem=rs_recv.at[i, index],
            device_id={"head": device},
            device_id_type=MESH,
        )

    def x1(i):
        return (
            rs_copy(i, 0, px.at[i, xo, pl.ds(0, piece)], rx1.at[i, 0], right),
            rs_copy(i, 1, px.at[i, xo, pl.ds(piece, piece)], rx1.at[i, 1], left),
        )

    def x2(i):
        return (
            rs_copy(i, 2, px.at[i, xr], rx2.at[i, 0], right),
            rs_copy(i, 3, px.at[i, xl], rx2.at[i, 1], left),
        )

    def x3(i):
        return (rs_copy(i, 4, sx.at[i], rx3.at[i], ypair),)

    def y1(i):
        return (rs_copy(i, 5, py.at[i, 1 - yl], ry1.at[i], ypair),)

    def y2(i):
        return (
            rs_copy(i, 6, py.at[i, yl, xo, pl.ds(0, piece // 2)], ry2.at[i, 0], right),
            rs_copy(i, 7, py.at[i, yl, xo, pl.ds(piece // 2, piece // 2)], ry2.at[i, 1], left),
        )

    def y3(i):
        return (
            rs_copy(i, 8, py.at[i, yl, xr], ry3.at[i, 0], right),
            rs_copy(i, 9, py.at[i, yl, xl], ry3.at[i, 1], left),
        )

    def start(copies):
        for copy in copies:
            copy.start()

    def landed(copies):
        for copy in copies:
            copy.wait_recv()

    def f32(value):
        return value.astype(jnp.float32)

    def bf16(value):
        return value.astype(jnp.bfloat16)

    def finish(i, shift, width, total):
        first = (i % GROUPS) * (CX + CY) + shift
        columns = pl.ds(pl.multiple_of(first, 128), width)
        mine = pl.ds(pl.multiple_of((i // GROUPS) * piece, piece), piece)
        gate = gatev[pl.ds(step, 1), columns]
        out_ref[mine, columns] = bf16(f32(resv[mine, columns]) + gate * total)

    low = pl.ds(0, piece)
    high = pl.ds(piece, piece)
    low2 = pl.ds(0, piece // 2)
    high2 = pl.ds(piece // 2, piece // 2)
    away = pl.ds(pl.multiple_of((1 - yl) * piece, piece), piece)
    kept = pl.ds(pl.multiple_of(yl * piece, piece), piece)

    def stage(s, later):
        slot = later % 8

        @pl.when(s < UNITS)
        def _():
            i = s
            half = i // GROUPS
            first = pl.multiple_of((i % GROUPS) * (CX + CY), 128)
            second = pl.multiple_of(first + CX, 128)
            wide = jnp.dot(
                att[half], wv[:, pl.ds(second, CY)], preferred_element_type=jnp.float32
            )
            wide = bf16(wide).reshape(X_RING, 2, piece, CY)
            py[i, 0] = wide[:, 0]
            py[i, 1] = wide[:, 1]
            start(y1(i))
            wide = jnp.dot(
                att[half], wv[:, pl.ds(first, CX)], preferred_element_type=jnp.float32
            )
            px[i] = bf16(wide).reshape(X_RING, 2 * piece, CX)
            start(x1(i))

        @pl.when(jnp.logical_and(s < BLOCKS - AT_ONCE, r >= slot))
        def _():
            attend(slot, 1)

        @pl.when(s == BLOCKS - AT_ONCE)
        def _():
            settle(1)

        @pl.when(jnp.logical_and(s >= LAG, s < UNITS + LAG))
        def _():
            i = s - LAG
            landed(x1(i))
            px[i, xr, low] = bf16(f32(px[i, xr, low]) + f32(rx1[i, 0]))
            px[i, xl, high] = bf16(f32(px[i, xl, high]) + f32(rx1[i, 1]))
            start(x2(i))
            landed(y1(i))
            py[i, yl] = bf16(f32(py[i, yl]) + f32(ry1[i]))
            start(y2(i))

        @pl.when(jnp.logical_and(s >= 2 * LAG, s < UNITS + 2 * LAG))
        def _():
            i = s - 2 * LAG
            landed(x2(i))
            sx[i] = bf16(
                f32(px[i, x, away]) + f32(rx2[i, 0, away]) + f32(rx2[i, 1, away])
            )
            start(x3(i))
            hx[i] = f32(px[i, x, kept]) + f32(rx2[i, 0, kept]) + f32(rx2[i, 1, kept])
            landed(y2(i))
            py[i, yl, xr, low2] = bf16(f32(py[i, yl, xr, low2]) + f32(ry2[i, 0]))
            py[i, yl, xl, high2] = bf16(f32(py[i, yl, xl, high2]) + f32(ry2[i, 1]))
            start(y3(i))

        @pl.when(s >= 3 * LAG)
        def _():
            i = s - 3 * LAG
            landed(x3(i))
            finish(i, 0, CX, hx[i] + f32(rx3[i]))
            landed(y3(i))
            total = f32(py[i, yl, x]) + f32(ry3[i, 0]) + f32(ry3[i, 1])
            finish(i, CX, CY, total)

        return later // 8

    lax.fori_loop(0, UNITS + 3 * LAG, stage, pick(orders[0][AT_ONCE:], orders[1][AT_ONCE:]))

    for index, (source, condition, target, span) in enumerate(routes):

        @pl.when(jnp.logical_and(condition, r >= source))
        def _(index=index, source=source, target=target, span=span):
            for part in (0, 1):
                kv_copy(index, part, source, target, span).wait_send()

    def drain(i, carry):
        for copies in (x1(i), x2(i), x3(i), y1(i), y2(i), y3(i)):
            for copy in copies:
                copy.wait_send()
        return carry

    lax.fori_loop(0, UNITS, drain, 0)


def on_device(q, k, v, w, residual, gate_table, noise_step, older_count):
    rows, width = q.shape
    heads = width // HEAD_SIZE
    half_rows = rows // HALVES
    piece = residual.shape[0] // HALVES
    q = q.reshape(half_rows // piece, HALVES, piece, width)
    any_space = pl.BlockSpec(memory_space=pl.ANY)
    smem = pl.BlockSpec(memory_space=pltpu.SMEM)
    bf, f3 = jnp.bfloat16, jnp.float32
    flops = 2 * rows * width * (w.shape[1] + 2 * BLOCKS * rows)
    return pl.pallas_call(
        kernel,
        out_shape=pltpu.VMEM(residual.shape, residual.dtype),
        in_specs=[any_space] * 6 + [smem] * 2,
        out_specs=pl.BlockSpec(memory_space=pltpu.VMEM),
        scratch_shapes=[
            pltpu.VMEM((BLOCKS, 2, rows, HEAD_SIZE), bf),
            pltpu.VMEM((rows, 2 * HEAD_SIZE), bf),
            pltpu.VMEM((HALVES, half_rows // piece, piece, width), bf),
            pltpu.VMEM(w.shape, bf),
            pltpu.VMEM(residual.shape, bf),
            pltpu.VMEM(gate_table.shape, f3),
            pltpu.VMEM((HALVES, heads, half_rows, 128), f3),
            pltpu.VMEM((HALVES, heads, half_rows, 2 * HEAD_SIZE), f3),
            pltpu.VMEM((HALVES, half_rows, width), bf),
            pltpu.VMEM((UNITS, X_RING, 2 * piece, CX), bf),
            pltpu.VMEM((UNITS, 2, piece, CX), bf),
            pltpu.VMEM((UNITS, 2, 2 * piece, CX), bf),
            pltpu.VMEM((UNITS, piece, CX), bf),
            pltpu.VMEM((UNITS, piece, CX), f3),
            pltpu.VMEM((UNITS, piece, CX), bf),
            pltpu.VMEM((UNITS, 2, X_RING, piece, CY), bf),
            pltpu.VMEM((UNITS, X_RING, piece, CY), bf),
            pltpu.VMEM((UNITS, 2, piece // 2, CY), bf),
            pltpu.VMEM((UNITS, 2, piece, CY), bf),
            pltpu.SemaphoreType.DMA((7,)),
            pltpu.SemaphoreType.DMA((9, 2)),
            pltpu.SemaphoreType.DMA((BLOCKS, 2)),
            pltpu.SemaphoreType.DMA((UNITS, 10)),
            pltpu.SemaphoreType.DMA((UNITS, 10)),
        ],
        compiler_params=pltpu.CompilerParams(
            collective_id=0, has_side_effects=True, vmem_limit_bytes=60 * 1024 * 1024
        ),
        cost_estimate=pl.CostEstimate(
            flops=flops,
            bytes_accessed=2 * w.size,
            transcendentals=rows * BLOCKS * rows * heads,
        ),
    )(q, k, v, w, residual, gate_table, noise_step, older_count)


def solution(mesh):
    in_specs = (
        P("span", "head"),
        P("span", "head"),
        P("span", "head"),
        P("head", None),
        P(("span", "head"), None),
        P(),
        P(),
        P(),
    )
    out_specs = P(("span", "head"), None)
    return jax.shard_map(
        on_device, mesh=mesh, in_specs=in_specs, out_specs=out_specs, check_vma=False
    )
```
